32 devices in a mesh: rep: 8 (over z, y), grp: 4 (over x, core).
Axes of the slice: x: 2, y: 2, z: 4, core: 2. Of those that a mesh axis runs over, the one named last changes fastest.
Arguments:
- layer_input: bfloat16 [8, 1536, 1024], P('rep', 'grp'), may hold values from -4 to 4
- branch: int32 [8, 2], P('rep'), may hold values from 192 to 768, as said below
- attention_gain: bfloat16 [1024], P('grp'), may hold values from 0.5 to 1.5
- factor_weight: bfloat16 [1024, 800], P('grp'), may hold values from -0.3125 to 0.3125
- output_weight: bfloat16 [1024, 1024], P('grp'), may hold values from -0.375 to 0.375
- feed_gain: bfloat16 [1024], P('grp'), may hold values from 0.5 to 1.5
- gate_weight: bfloat16 [1024, 2816], P('grp'), may hold values from -0.1875 to 0.1875
- up_weight: bfloat16 [1024, 2816], P('grp'), may hold values from -0.1875 to 0.1875
- down_weight: bfloat16 [2816, 1024], P('grp'), may hold values from -0.109375 to 0.109375
- cotangent: bfloat16 [8, 1536, 1024], P('rep', 'grp'), may hold values from -4 to 4
Outputs:
- layer_output: bfloat16 [8, 1536, 1024], P('rep', 'grp')
- input_grad: float32 [8, 1536, 1024], P('rep', 'grp')
- attention_gain_grad: float32 [1024], P('grp')
- factor_weight_grad: float32 [1024, 800], P('grp')
- output_weight_grad: float32 [1024, 1024], P('grp')
- feed_gain_grad: float32 [1024], P('grp')
- gate_weight_grad: float32 [1024, 2816], P('grp')
- up_weight_grad: float32 [1024, 2816], P('grp')
- down_weight_grad: float32 [2816, 1024], P('grp')
The draws below stay inside these ranges and needn't reach their ends.
Inputs may be any that keep to these rules, and one draw needn't show every extreme that they name: Continuation c of group g follows the first branch[g, c] prompt tokens; in every group one continuation follows all 768.
All inputs are finite; a program needn't handle non-finite values.
Results may differ from the reference program's by a relative error of at most 0.024.
The reference program's roundings to bfloat16 on the way count: a program that leaves them out, or rounds other values in their place, can miss the bound.
Values may be sent and summed in bfloat16 or wider, within the bound.
No kernel may reach another device: no remote copies, remote signals or barrier semaphores. Data moves between devices by JAX's collectives and lax.ppermute only.
A program may use at most 128 MiB of HBM per device.

```python
import jax
import jax.numpy as jnp
from jax import lax

D = 1024
HEADS = 16
HDIM = 64
QRANK = 6
KRANK = 2
FF = 2816
TOK_DEV = 384
GROUPS = 8
GTOK = 1536
PLEN = 768
NCONT = 2
FAC = 800


def draw_branch(key, part):
    first_key, second_key = jax.random.split(jax.random.fold_in(key, 17))
    lengths = jax.random.randint(first_key, (GROUPS, NCONT), PLEN // 4, PLEN + 1)
    full_place = jax.random.randint(second_key, (GROUPS, 1), 0, NCONT)
    return jnp.where(jnp.arange(NCONT)[None, :] == full_place, PLEN, lengths).astype(jnp.int32)


def level_of(own_key, dims, cuts, smallest, high):
    loudness, own = 1.0, jax.random.fold_in(own_key, 6)
    for dim, shards_of in cuts:
        steps = jnp.exp(jax.random.uniform(jax.random.fold_in(own, dim), (shards_of,), jnp.float32, smallest / len(cuts), high / len(cuts)))
        loudness = loudness * jnp.repeat(steps, dims[dim] // shards_of).reshape([-1 if axis == dim else 1 for axis in range(len(dims))])
    return loudness


def bell_draw(rng, extent, width, most, cuts=(), kind=jnp.bfloat16):
    factor_of = level_of(rng, extent, cuts, -0.22, 0.18) if cuts else 1.0
    values = jax.random.normal(rng, extent, jnp.float32) * width * factor_of
    return jnp.minimum(jnp.maximum(values, -most), most).astype(kind)


def setup_inputs(seed: int = 0) -> dict:
    arg_keys = jax.random.split(jax.random.key(seed), 11)
    layer_input = bell_draw(arg_keys[0], (GROUPS, GTOK, D), 1.0, 4.0, ((0, 8), (1, 4)))
    branch = draw_branch(jax.random.fold_in(arg_keys[10], 71), 0)
    attention_gain = jnp.clip(1.0 + 0.1 * jax.random.normal(arg_keys[2], (D,), jnp.float32), 0.5, 1.5).astype(jnp.bfloat16)
    factor_weight = bell_draw(arg_keys[3], (D, FAC), (2 * D // 5) ** -0.5, 0.3125, ((0, 4),))
    output_weight = bell_draw(arg_keys[4], (HEADS * HDIM, D), (D // 4) ** -0.5, 0.375, ((0, 4),))
    feed_gain = jnp.clip(1.0 + 0.1 * jax.random.normal(arg_keys[5], (D,), jnp.float32), 0.5, 1.5).astype(jnp.bfloat16)
    gate_weight = bell_draw(arg_keys[6], (D, FF), D ** -0.5, 0.1875, ((0, 4),))
    up_weight = bell_draw(arg_keys[7], (D, FF), D ** -0.5, 0.1875, ((0, 4),))
    down_weight = bell_draw(arg_keys[8], (FF, D), FF ** -0.5, 0.109375, ((0, 4),))
    cotangent = bell_draw(arg_keys[9], (GROUPS, GTOK, D), 1.0, 4.0, ((0, 8), (1, 4)))
    return dict(layer_input=layer_input, branch=branch, attention_gain=attention_gain, factor_weight=factor_weight, output_weight=output_weight, feed_gain=feed_gain, gate_weight=gate_weight, up_weight=up_weight, down_weight=down_weight, cotangent=cotangent)


@jax.custom_vjp
def low(v):
    return lax.optimization_barrier(v.astype(jnp.bfloat16)).astype(jnp.float32)

@jax.custom_vjp
def low_back(v):
    return v

def low_keep(v):
    return (low(v), None)

def low_pass(kept, grad):
    return (grad,)

def back_keep(v):
    return (v, None)

def back_low(kept, grad):
    return (low(grad),)
low.defvjp(low_keep, low_pass)
low_back.defvjp(back_keep, back_low)
highest = lax.Precision.HIGHEST

def product(left_side, right_side):
    return jnp.dot(left_side, right_side, precision=highest, preferred_element_type=jnp.float32)

def rms_norm(values, gain_vector):
    return values * lax.rsqrt(lax.optimization_barrier(jnp.mean(values * values, axis=-1, keepdims=True)) + 1e-05) * gain_vector

def angles(positions, half_width):
    freqs = 10000.0 ** (-jnp.arange(half_width).astype(jnp.float32) / half_width)
    phase = positions.astype(jnp.float32)[:, None] * freqs[None, :]
    return (jnp.cos(phase), jnp.sin(phase))

def rotate(matrix, cosine, sine, ranks):
    half_cols = matrix.shape[1] // (2 * ranks)
    pieces = matrix.reshape(matrix.shape[0], ranks, 2, half_cols)
    first_half = pieces[:, :, 0]
    second_half = pieces[:, :, 1]
    cos_wide = cosine[:, None, :]
    sin_wide = sine[:, None, :]
    turned = jnp.stack([first_half * cos_wide - second_half * sin_wide, second_half * cos_wide + first_half * sin_wide], axis=2)
    return turned.reshape(matrix.shape)

def cut_points():
    first_cut = QRANK * HEADS
    second_cut = first_cut + QRANK * HDIM
    third_cut = second_cut + KRANK * HEADS
    fourth_cut = third_cut + KRANK * HDIM
    fifth_cut = fourth_cut + KRANK * HEADS
    return (first_cut, second_cut, third_cut, fourth_cut, fifth_cut)

def turn_factors(values, cosine, sine):
    cuts = cut_points()
    return jnp.concatenate([values[:, :cuts[0]], rotate(values[:, cuts[0]:cuts[1]], cosine, sine, QRANK), values[:, cuts[1]:cuts[2]], rotate(values[:, cuts[2]:cuts[3]], cosine, sine, KRANK), values[:, cuts[3]:]], axis=1)

def expand(head_part, dim_part, ranks):
    tokens_here = head_part.shape[0]
    left_factor = head_part.reshape(tokens_here, ranks, HEADS)
    right_factor = dim_part.reshape(tokens_here, ranks, HDIM)
    return jnp.einsum('nrh,nrd->nhd', left_factor, right_factor, precision=highest) / ranks

def geometry(table):
    index = jnp.arange(GTOK).astype(jnp.int32)
    inside = index < PLEN
    segment = jnp.where(inside, -1, (index - PLEN) // TOK_DEV).astype(jnp.int32)
    chosen = table[jnp.maximum(segment, 0)]
    position = jnp.where(inside, index, chosen + (index - PLEN) % TOK_DEV)
    limit = jnp.where(inside, 0, chosen)
    return (index, segment, position, limit)

def residual_block(inputs, attention_gain, factor_weight, output_weight, feed_gain, gate_weight, up_weight, down_weight, index, segment, position, limit):
    hidden_one = low(rms_norm(inputs, attention_gain))
    raw_factors = low_back(product(hidden_one, factor_weight))
    cosine, sine = angles(position, HDIM // 2)
    factors = low(turn_factors(raw_factors, cosine, sine))
    cuts = cut_points()
    queries = low(expand(factors[:, :cuts[0]], factors[:, cuts[0]:cuts[1]], QRANK))
    keys_all = low(expand(factors[:, cuts[1]:cuts[2]], factors[:, cuts[2]:cuts[3]], KRANK))
    values_all = low(expand(factors[:, cuts[3]:cuts[4]], factors[:, cuts[4]:], KRANK))
    block_rows = 512 if GTOK % 512 == 0 else GTOK
    block_count = GTOK // block_rows

    def attend(element):
        query_part, query_index, query_seg, query_lim = element
        logits = low_back(jnp.einsum('qhd,khd->hqk', query_part, keys_all, precision=highest) * HDIM ** (-0.5))
        same_line = (segment[None, :] == query_seg[:, None]) & (index[None, :] <= query_index[:, None])
        from_prompt = (segment[None, :] == -1) & (index[None, :] < query_lim[:, None])
        logits = jnp.where((same_line | from_prompt)[None], logits, -1e+30)
        highest_score = lax.optimization_barrier(jnp.max(logits, axis=-1, keepdims=True))
        weights_now = jnp.exp(logits - highest_score)
        probs = low(weights_now / lax.optimization_barrier(jnp.sum(weights_now, axis=-1, keepdims=True)))
        return jnp.einsum('hqk,khd->qhd', probs, values_all, precision=highest)
    mixed = lax.map(jax.checkpoint(attend), (queries.reshape(block_count, block_rows, HEADS, HDIM), index.reshape(block_count, block_rows), segment.reshape(block_count, block_rows), limit.reshape(block_count, block_rows)))
    attended = low(low_back(mixed.reshape(GTOK, HEADS * HDIM)))
    middle = inputs + low_back(product(attended, output_weight))
    hidden_two = low(rms_norm(middle, feed_gain))
    gate_values = low_back(product(hidden_two, gate_weight))
    up_values = low_back(product(hidden_two, up_weight))
    active = low(gate_values * jax.nn.sigmoid(gate_values) * up_values)
    return middle + low_back(product(active, down_weight))

def reference(layer_input, branch, attention_gain, factor_weight, output_weight, feed_gain, gate_weight, up_weight, down_weight, cotangent):
    weights_all = tuple((weight.astype(jnp.float32) for weight in (attention_gain, factor_weight, output_weight, feed_gain, gate_weight, up_weight, down_weight)))

    def one_group(totals, element):
        group_input, table, upstream = element
        index, segment, position, limit = geometry(table)

        def forward(values, *params):
            return residual_block(values, *params, index, segment, position, limit)
        result, pull = jax.vjp(forward, group_input.astype(jnp.float32), *weights_all)
        grads = pull(upstream.astype(jnp.float32))
        totals = tuple((running + grad for running, grad in zip(totals, grads[1:])))
        return (totals, (result.astype(jnp.bfloat16), grads[0]))
    start_totals = tuple((jnp.zeros(weight.shape, jnp.float32) for weight in weights_all))
    totals, (results, input_grads) = lax.scan(one_group, start_totals, (layer_input, branch, cotangent))
    return (results, input_grads, totals[0], totals[1], totals[2], totals[3], totals[4], totals[5], totals[6])
```

```python
import functools

import jax
import jax.numpy as jnp
from jax import lax
from jax.experimental import pallas as pl
from jax.experimental.pallas import tpu as pltpu
from jax.sharding import PartitionSpec as P

HEADS = 16
HDIM = 64
QRANK = 6
KRANK = 2
PAIRS = HEADS // 2
CUT_Q = QRANK * HEADS
CUT_QB = CUT_Q + QRANK * HDIM
CUT_K = CUT_QB + KRANK * HEADS
CUT_KB = CUT_K + KRANK * HDIM
CUT_V = CUT_KB + KRANK * HEADS
CUT_VB = CUT_V + KRANK * HDIM

bf16 = jnp.bfloat16
f32 = jnp.float32


def dot(spec, left, right):
    return jnp.einsum(spec, left, right, preferred_element_type=f32)


def rms_scale(values):
    return lax.rsqrt(jnp.mean(values * values, axis=-1, keepdims=True) + 1e-05)


def norm_back(grad_hidden, normed, scale, gain):
    grad_normed = grad_hidden * gain
    gain_grad = jnp.sum(grad_hidden * normed, axis=0)
    grad_values = scale * (
        grad_normed - normed * jnp.mean(grad_normed * normed, axis=-1, keepdims=True)
    )
    return gain_grad, grad_values


def swap(value, axis, mask):
    size = lax.axis_size(axis)
    return lax.ppermute(value, axis, [(j, j ^ mask) for j in range(size)])


def bits_down(size):
    mask, out = size // 2, []
    while mask:
        out.append(mask)
        mask //= 2
    return out


def gather_rel(block, axis="grp"):
    have = {0: block}
    for mask in bits_down(lax.axis_size(axis)):
        for s in sorted(have):
            have[s ^ mask] = swap(have[s], axis, mask)
    return [have[s] for s in range(len(have))]


def scatter_rel(parts, axis="grp"):
    parts = dict(enumerate(parts))
    for mask in reversed(bits_down(lax.axis_size(axis))):
        for s in sorted(parts):
            if not s & mask:
                moved = swap(parts[s | mask].astype(bf16), axis, mask)
                parts[s] = parts[s].astype(f32) + moved.astype(f32)
                del parts[s | mask]
    return parts[0]


def exchange_rel(parts, axis="grp"):
    return [part if s == 0 else swap(part, axis, s) for s, part in enumerate(parts)]


def in_order(blocks, own, axis):
    stacked = jnp.stack(blocks)
    return jnp.concatenate(
        [lax.dynamic_index_in_dim(stacked, own ^ j, 0, False) for j in range(len(blocks))],
        axis=axis,
    )


def rel_rows(matrix, own, count):
    pieces = matrix.reshape(count, matrix.shape[0] // count, matrix.shape[1])
    return [lax.dynamic_index_in_dim(pieces, own ^ s, 0, False) for s in range(count)]


def small_sum(value, axis="rep"):
    own = lax.axis_index(axis)
    masks = bits_down(lax.axis_size(axis))[::-1]
    for mask in masks:
        half = value.shape[0] // 2
        upper = (own // mask) % 2 == 1
        keep = jnp.where(upper, value[half:], value[:half])
        send = jnp.where(upper, value[:half], value[half:])
        value = (keep.astype(f32) + swap(send, axis, mask).astype(f32)).astype(bf16)
    for mask in masks[::-1]:
        upper = (own // mask) % 2 == 1
        other = swap(value, axis, mask)
        value = jnp.where(
            upper,
            jnp.concatenate([other, value], axis=0),
            jnp.concatenate([value, other], axis=0),
        )
    return value


def turn(block, cosine, sine):
    rows, tokens = block.shape
    pieces = block.reshape(rows // HDIM, 2, HDIM // 2, tokens)
    first, second = pieces[:, 0], pieces[:, 1]
    return jnp.stack(
        [first * cosine - second * sine, second * cosine + first * sine], axis=1
    ).reshape(rows, tokens)


def turn_factors(values, cosine, sine):
    return jnp.concatenate(
        [
            values[:CUT_Q],
            turn(values[CUT_Q:CUT_QB], cosine, sine),
            values[CUT_QB:CUT_K],
            turn(values[CUT_K:CUT_KB], cosine, sine),
            values[CUT_KB:],
        ],
        axis=0,
    )


def by_pair(heads_part, ranks):
    tokens = heads_part.shape[1]
    return (
        heads_part.reshape(ranks, PAIRS, 2, tokens)
        .transpose(1, 2, 0, 3)
        .reshape(PAIRS, 2 * ranks, tokens)
    )


def from_pair(parts, ranks):
    tokens = parts.shape[2]
    return (
        parts.reshape(PAIRS, 2, ranks, tokens)
        .transpose(2, 0, 1, 3)
        .reshape(ranks * HEADS, tokens)
    )


def expand(a_ref, b_ref, head, ranks):
    total = None
    for r in range(ranks):
        term = b_ref[r * HDIM : (r + 1) * HDIM, :] * a_ref[0, head * ranks + r, :][None, :]
        total = term if total is None else total + term
    return (total / ranks).astype(bf16)


def fill_bias(limit_ref, row_ref, square_ref):
    @pl.when(pl.program_id(0) == 0)
    def _():
        column = lax.broadcasted_iota(jnp.int32, row_ref.shape, 1)
        row_ref[...] = jnp.where(column < limit_ref[0], 0.0, -1e30)
        rows = lax.broadcasted_iota(jnp.int32, square_ref.shape, 0)
        columns = lax.broadcasted_iota(jnp.int32, square_ref.shape, 1)
        square_ref[...] = jnp.where(columns <= rows, 0.0, -1e30)


def rows_by_rows(left, right):
    return lax.dot_general(left, right, (((1,), (1,)), ((), ())), preferred_element_type=f32)


def plain(left, right):
    return jnp.dot(left, right, preferred_element_type=f32)


def forward_kernel(
    prefix, limit_ref, aq, bq, ak, bk, av, bv, out_ref, log_ref, row_ref, square_ref
):
    fill_bias(limit_ref, row_ref, square_ref)
    outs, logs = [], []
    for head in range(2):
        q = (expand(aq, bq, head, QRANK).astype(f32) * HDIM**-0.5).T.astype(bf16)
        k = expand(ak, bk, head, KRANK)
        v = expand(av, bv, head, KRANK)
        s_far = plain(q, k[:, :prefix]) + row_ref[0:1, :]
        s_own = plain(q, k[:, prefix:]) + square_ref[...]
        top = jnp.maximum(
            jnp.max(s_far, axis=1, keepdims=True), jnp.max(s_own, axis=1, keepdims=True)
        )
        e_far, e_own = jnp.exp(s_far - top), jnp.exp(s_own - top)
        mass = jnp.sum(e_far, axis=1, keepdims=True) + jnp.sum(e_own, axis=1, keepdims=True)
        share = 1.0 / mass
        outs.append(
            rows_by_rows((e_far * share).astype(bf16), v[:, :prefix])
            + rows_by_rows((e_own * share).astype(bf16), v[:, prefix:])
        )
        logs.append(jnp.broadcast_to(top + jnp.log(mass), (q.shape[0], HDIM)))
    out_ref[...] = jnp.concatenate(outs, axis=1).astype(bf16)
    log_ref[0] = jnp.concatenate(logs, axis=1)


def backward_kernel(
    prefix, limit_ref, aq, bq, ak, bk, av, bv, do_ref, o_ref, log_ref,
    daq, dbq, dak, dbk, dav, dbv, row_ref, square_ref,
):
    fill_bias(limit_ref, row_ref, square_ref)

    @pl.when(pl.program_id(0) == 0)
    def _():
        dbq[...] = jnp.zeros_like(dbq)
        dbk[...] = jnp.zeros_like(dbk)
        dbv[...] = jnp.zeros_like(dbv)

    def factor_grads(grad, head, ranks, a_ref, b_ref, da_ref, db_ref):
        grad = grad / ranks
        for r in range(ranks):
            rows = slice(r * HDIM, (r + 1) * HDIM)
            spot = head * ranks + r
            da_ref[0, spot : spot + 1, :] = jnp.sum(grad * b_ref[rows, :], axis=0, keepdims=True)
            db_ref[rows, :] += grad * a_ref[0, spot, :][None, :]

    do_all = do_ref[...]
    do_turned = do_all.astype(f32).T.astype(bf16)
    products = do_all.astype(f32) * o_ref[...].astype(f32)
    for head in range(2):
        cols = slice(head * HDIM, (head + 1) * HDIM)
        q_turned = expand(aq, bq, head, QRANK).astype(f32) * HDIM**-0.5
        q = q_turned.T.astype(bf16)
        q_turned = q_turned.astype(bf16)
        k = expand(ak, bk, head, KRANK)
        v = expand(av, bv, head, KRANK)
        log_total = log_ref[0][:, head * HDIM : head * HDIM + 1]
        delta = jnp.sum(products[:, cols], axis=1, keepdims=True)
        do_head = do_all[:, cols]
        grad_q = None
        grads_k, grads_v = [], []
        for low, high, bias in (
            (0, prefix, row_ref[0:1, :]),
            (prefix, k.shape[1], square_ref[...]),
        ):
            k_part, v_part = k[:, low:high], v[:, low:high]
            probs = jnp.exp(plain(q, k_part) + bias - log_total)
            grad_s = (probs * (plain(do_head, v_part) - delta)).astype(bf16)
            part = rows_by_rows(grad_s, k_part)
            grad_q = part if grad_q is None else grad_q + part
            grads_k.append(plain(q_turned, grad_s))
            grads_v.append(plain(do_turned[cols], probs.astype(bf16)))
        factor_grads((grad_q * HDIM**-0.5).T, head, QRANK, aq, bq, daq, dbq)
        factor_grads(jnp.concatenate(grads_k, axis=1), head, KRANK, ak, bk, dak, dbk)
        factor_grads(jnp.concatenate(grads_v, axis=1), head, KRANK, av, bv, dav, dbv)


def pair_spec(rows, tokens):
    return pl.BlockSpec((1, rows, tokens), lambda p: (p, 0, 0))


def whole_spec(rows, tokens):
    return pl.BlockSpec((rows, tokens), lambda p: (0, 0))


def attention_specs(tokens, keys):
    return [
        pl.BlockSpec(memory_space=pltpu.SMEM),
        pair_spec(2 * QRANK, tokens),
        whole_spec(QRANK * HDIM, tokens),
        pair_spec(2 * KRANK, keys),
        whole_spec(KRANK * HDIM, keys),
        pair_spec(2 * KRANK, keys),
        whole_spec(KRANK * HDIM, keys),
    ]


def attention_forward(limit, factors, tokens, keys):
    prefix = keys - tokens
    column = pl.BlockSpec((tokens, 2 * HDIM), lambda p: (0, p))
    return pl.pallas_call(
        functools.partial(forward_kernel, prefix),
        grid=(PAIRS,),
        in_specs=attention_specs(tokens, keys),
        out_specs=[column, pair_spec(tokens, 2 * HDIM)],
        out_shape=[
            jax.ShapeDtypeStruct((tokens, HEADS * HDIM), bf16),
            jax.ShapeDtypeStruct((PAIRS, tokens, 2 * HDIM), f32),
        ],
        scratch_shapes=[pltpu.VMEM((8, prefix), f32), pltpu.VMEM((tokens, tokens), f32)],
        cost_estimate=pl.CostEstimate(
            flops=16 * HEADS * tokens * keys * HDIM,
            bytes_accessed=8 * tokens * HEADS * HDIM,
            transcendentals=HEADS * tokens * keys,
        ),
        name="attend",
    )(limit, *factors)


def attention_backward(limit, factors, do, o, logs, tokens, keys):
    prefix = keys - tokens
    column = pl.BlockSpec((tokens, 2 * HDIM), lambda p: (0, p))
    shapes = [
        (PAIRS, 2 * QRANK, tokens),
        (QRANK * HDIM, tokens),
        (PAIRS, 2 * KRANK, keys),
        (KRANK * HDIM, keys),
        (PAIRS, 2 * KRANK, keys),
        (KRANK * HDIM, keys),
    ]
    return pl.pallas_call(
        functools.partial(backward_kernel, prefix),
        grid=(PAIRS,),
        in_specs=attention_specs(tokens, keys)
        + [column, column, pair_spec(tokens, 2 * HDIM)],
        out_specs=attention_specs(tokens, keys)[1:],
        out_shape=[jax.ShapeDtypeStruct(shape, f32) for shape in shapes],
        scratch_shapes=[pltpu.VMEM((8, prefix), f32), pltpu.VMEM((tokens, tokens), f32)],
        cost_estimate=pl.CostEstimate(
            flops=40 * HEADS * tokens * keys * HDIM,
            bytes_accessed=16 * tokens * HEADS * HDIM,
            transcendentals=HEADS * tokens * keys,
        ),
        name="attend_back",
    )(limit, *factors, do, o, logs)


def local(
    layer_input,
    branch,
    attention_gain,
    factor_weight,
    output_weight,
    feed_gain,
    gate_weight,
    up_weight,
    down_weight,
    cotangent,
):
    count = lax.axis_size("grp")
    own = lax.axis_index("grp")
    half = count // 2
    tokens, width = layer_input.shape[1:]
    rows = factor_weight.shape[0]
    fac = factor_weight.shape[1]
    feed = down_weight.shape[0]
    prefix = tokens * half
    keys = prefix + tokens
    upstream = cotangent[0]

    packed = jnp.concatenate(
        [factor_weight, attention_gain[:, None], feed_gain[:, None]], axis=1
    )
    packed = in_order(gather_rel(packed), own, 0)
    factor_full = packed[:, :fac]
    gain_one = packed[:, fac].astype(f32)
    gain_two = packed[:, fac + 1].astype(f32)

    lane = own - half
    chosen = jnp.sum(jnp.where(jnp.arange(branch.shape[1]) == lane, branch[0], 0))
    is_prompt = own < half
    start = jnp.where(is_prompt, own * tokens, chosen)
    positions = start + jnp.arange(tokens, dtype=jnp.int32)
    limit = start.astype(jnp.int32).reshape(1)
    freqs = 10000.0 ** (-jnp.arange(HDIM // 2).astype(f32) / (HDIM // 2))
    phase = freqs[:, None] * positions.astype(f32)[None, :]
    cosine, sine = jnp.cos(phase), jnp.sin(phase)

    residual_in = layer_input[0].astype(f32)
    scale_one = rms_scale(residual_in)
    normed_one = residual_in * scale_one
    hidden_one = (normed_one * gain_one).astype(bf16)
    raw = dot("df,td->ft", factor_full, hidden_one)
    factors = turn_factors(raw, cosine, sine).astype(bf16)

    table = factors[CUT_QB:]
    arrived = lax.ppermute(table, "grp", [(j, j + half) for j in range(half)])
    have = {0: jnp.where(is_prompt, table, arrived)}
    for mask in bits_down(half):
        for s in sorted(have):
            have[s ^ mask] = swap(have[s], "grp", mask)
    low_own = own % half
    table_all = jnp.concatenate(
        [in_order([have[s] for s in range(half)], low_own, 1), table], axis=1
    ).astype(f32)
    o_k, o_kb, o_v = CUT_K - CUT_QB, CUT_KB - CUT_QB, CUT_V - CUT_QB
    attention_in = (
        by_pair(factors[:CUT_Q].astype(f32), QRANK),
        factors[CUT_Q:CUT_QB].astype(f32),
        by_pair(table_all[:o_k], KRANK),
        table_all[o_k:o_kb],
        by_pair(table_all[o_kb:o_v], KRANK),
        table_all[o_v:],
    )
    attended, logs = attention_forward(limit, attention_in, tokens, keys)

    def own_columns(weight):
        pieces = weight.reshape(rows, count, feed).transpose(1, 0, 2)
        parts = [lax.dynamic_index_in_dim(pieces, own ^ s, 0, False) for s in range(count)]
        return in_order(exchange_rel(parts), own, 0)

    output_full = in_order(gather_rel(output_weight), own, 0)
    gate_full = own_columns(gate_weight)
    up_full = own_columns(up_weight)
    upstream_all = jnp.concatenate(gather_rel(upstream), axis=0)

    middle = residual_in + dot("tf,fd->td", attended, output_full)
    scale_two = rms_scale(middle)
    normed_two = middle * scale_two
    hidden_two = (normed_two * gain_two).astype(bf16)
    hidden_all = jnp.concatenate(gather_rel(hidden_two), axis=0)

    active_grad = dot("td,fd->tf", upstream_all, down_weight)
    gate = dot("td,df->tf", hidden_all, gate_full)
    up = dot("td,df->tf", hidden_all, up_full)
    sig = jax.nn.sigmoid(gate)
    active = (gate * sig * up).astype(bf16)
    gate_grad = (active_grad * up * sig * (1.0 + gate * (1.0 - sig))).astype(bf16)
    up_grad = (active_grad * gate * sig).astype(bf16)

    def blocks(matrix):
        return [matrix[s * tokens : (s + 1) * tokens] for s in range(count)]

    hidden_grad = dot("tf,df->td", gate_grad, gate_full) + dot("tf,df->td", up_grad, up_full)
    hidden_two_grad = scatter_rel(blocks(hidden_grad))
    result = middle + scatter_rel(blocks(dot("tf,fd->td", active, down_weight)))

    down_grad = dot("tf,td->fd", active, upstream_all).astype(bf16)
    gate_weight_grad = dot("td,tf->df", hidden_all, gate_grad).astype(bf16)
    up_weight_grad = dot("td,tf->df", hidden_all, up_grad).astype(bf16)

    def own_rows(grad):
        return jnp.stack(exchange_rel(rel_rows(grad, own, count)))

    gate_pieces = own_rows(gate_weight_grad)
    up_pieces = own_rows(up_weight_grad)

    feed_gain_grad, middle_grad = norm_back(hidden_two_grad, normed_two, scale_two, gain_two)
    middle_grad = middle_grad + upstream.astype(f32)
    branch_grad = middle_grad.astype(bf16)
    output_weight_grad = dot("tf,td->fd", attended, branch_grad)
    output_piece = scatter_rel(rel_rows(output_weight_grad, own, count)).astype(bf16)
    grad_heads = dot("td,fd->tf", branch_grad, output_full).astype(bf16)

    gate_sum, up_sum, down_sum, output_sum = lax.psum(
        (gate_pieces, up_pieces, down_grad, output_piece), "rep"
    )

    def final_columns(pieces):
        return in_order([pieces[s] for s in range(count)], own, 1).astype(f32)

    daq, dbq, dak, dbk, dav, dbv = attention_backward(
        limit, attention_in, grad_heads, attended, logs, tokens, keys
    )
    table_grad = jnp.concatenate(
        [from_pair(dak, KRANK), dbk, from_pair(dav, KRANK), dbv], axis=0
    )
    far = table_grad[:, :prefix].reshape(-1, half, tokens)
    far = far.transpose(1, 0, 2)
    parts = {s: lax.dynamic_index_in_dim(far, low_own ^ s, 0, False) for s in range(half)}
    for mask in reversed(bits_down(half)):
        for s in sorted(parts):
            if not s & mask:
                parts[s] = parts[s] + swap(parts[s | mask].astype(bf16), "grp", mask).astype(f32)
                del parts[s | mask]
    back = lax.ppermute(parts[0].astype(bf16), "grp", [(j + half, j) for j in range(half)])
    own_table = table_grad[:, prefix:] + jnp.where(is_prompt, parts[0] + back.astype(f32), 0.0)

    factor_grad = jnp.concatenate([from_pair(daq, QRANK), dbq, own_table], axis=0)
    raw_grad = turn_factors(factor_grad, cosine, -sine).astype(bf16)
    factor_weight_grad = dot("td,ft->df", hidden_one, raw_grad)
    hidden_one_grad = dot("ft,df->td", raw_grad, factor_full)
    attention_gain_grad, input_part = norm_back(hidden_one_grad, normed_one, scale_one, gain_one)
    input_grad = middle_grad + input_part

    tail = jnp.concatenate(
        [factor_weight_grad, attention_gain_grad[:, None], feed_gain_grad[:, None]], axis=1
    )
    tail = scatter_rel(rel_rows(tail, own, count)).astype(bf16)
    tail = small_sum(tail).astype(f32)

    return (
        result.astype(bf16)[None],
        input_grad[None],
        tail[:, fac],
        tail[:, :fac],
        output_sum.astype(f32),
        tail[:, fac + 1],
        final_columns(gate_sum),
        final_columns(up_sum),
        down_sum.astype(f32),
    )


def solution(mesh):
    specs = (
        P("rep", "grp", None),
        P("rep", None),
        P("grp"),
        P("grp", None),
        P("grp", None),
        P("grp"),
        P("grp", None),
        P("grp", None),
        P("grp", None),
        P("rep", "grp", None),
    )
    out_specs = (
        P("rep", "grp", None),
        P("rep", "grp", None),
        P("grp"),
        P("grp", None),
        P("grp", None),
        P("grp"),
        P("grp", None),
        P("grp", None),
        P("grp", None),
    )
    return jax.shard_map(local, mesh=mesh, in_specs=specs, out_specs=out_specs, check_vma=False)
```
